32 devices in a mesh: seq: 8 (over z, y), exp: 4 (over x, core).
Axes of the slice: x: 2, y: 2, z: 4, core: 2. Of those that a mesh axis runs over, the one named last changes fastest.
Arguments:
- projected: bfloat16 [3, 1024, 4096], P(None, 'seq', 'exp'), may hold values from -6 to 6
- stream: bfloat16 [1024, 4096], P('seq', 'exp'), may hold values from -6 to 6
- short_filter: float32 [3, 3, 4096], P(None, None, 'exp'), may hold values from -3.5 to 3.5
- long_filter: float32 [1024, 4096], P('seq', 'exp'), may hold values from -0.1875 to 0.1875
- skip_gain: float32 [4096], P('exp'), may hold values from 0.25 to 1.75
- norm_gain: float32 [4096], P('exp'), may hold values from 0.25 to 1.75
- gate_up: bfloat16 [16, 4096, 2, 1408], P('seq', 'exp'), may hold values from -0.125 to 0.125
- down_weight: bfloat16 [16, 1408, 4096], P('seq', None, 'exp'), may hold values from -0.15625 to 0.15625
- expert_ids: int32 [1024, 6], P('seq'), may hold values from 0 to 15, all different within a row; in each aligned block of 128 rows (0 to 127, 128 to 255, ...) at most 64 rows name the same one
- gate_weights: float32 [1024, 6], P('seq'), may hold values from 0.2 to 1
Outputs:
- mixed: bfloat16 [1024, 4096], P('seq', 'exp')
The draws below stay inside these ranges and needn't reach their ends.
Inputs may be any that keep to these rules, and one draw needn't show every extreme that they name: `expert_ids`: each row names 6 different experts. In each aligned block of 128 rows (the rows of one index of seq) no expert is named more than 64 times, a bound that some block reaches.
All inputs are finite; a program needn't handle non-finite values.
Results may differ from the reference program's by a relative error of at most 0.022.
Values may be sent and summed in bfloat16 or wider, within the bound.
No kernel may reach another device: no remote copies, remote signals or barrier semaphores. Data moves between devices by JAX's collectives and lax.ppermute only.
A program may use at most 192 MiB of HBM per device.

```python
import math
import jax
import jax.numpy as jnp
import numpy as np
from jax import lax

D = 4096
FF = 1408
TOP = 6
TAPS = 3
TOK_DEV = 128
LENGTH = 1024
EXPERTS = 16
CAP = 64
N_SEQ = 8
N_EXP = 4


def with_spikes(values, own_key, source, target, parts, factor):
    owner, partner = [(jnp.arange(values.shape[axis_at]) // (values.shape[axis_at] // parts)).reshape([-1 if axis == axis_at else 1 for axis in range(values.ndim)]) for axis_at in (source, target)]
    chosen = jax.random.permutation(own_key, parts)[partner]
    strong = (owner == chosen) | (owner == (partner + parts // 2) % parts)
    return jnp.where(strong, factor * values, values)


def steps_of(key, dims, shards, least, largest):
    level = 1.0
    for dim, blocks in shards:
        draws = jax.random.uniform(jax.random.fold_in(jax.random.fold_in(key, 6), dim), (blocks,), jnp.float32, least / len(shards), largest / len(shards))
        level = level * jnp.repeat(jnp.exp(draws), dims[dim] // blocks).reshape((-1,) + (1,) * (len(dims) - 1 - dim))
    return level


def routed_block(key, own, number, rows, count, top, limit, slope):
    ranking = jax.random.permutation(key, count)
    heavy_load, common = portions_of(count, rows * top, limit, slope, True), portions_of(count, rows * top, limit, slope, False)
    places = jnp.arange(count)

    def named(sizes, turn):
        used = int((sizes > 0).sum())
        fixed = max(1, used // 4)
        moved = fixed + (places - fixed + turn * (used - fixed)) % max(1, count - fixed)
        return jnp.zeros((count,), jnp.int32).at[ranking[jnp.where(places < fixed, places, moved)]].set(jnp.asarray(sizes, jnp.int32))

    sizes = jnp.where(number % 4 == 0, named(heavy_load, number // 4), named(common, number - number // 4 - 1))
    mixed = jax.random.permutation(jax.random.fold_in(own, 3), count)
    donor, receiver = mixed[0:count // 2 * 2:2], mixed[1:count // 2 * 2:2]
    room = jnp.minimum(sizes[donor] - 1, limit - sizes[receiver]) // 2
    room = jnp.where((donor == ranking[0]) | (receiver == ranking[0]) | (sizes[receiver] == 0), 0, jnp.maximum(room, 0))
    moved = jax.random.randint(jax.random.fold_in(own, 4), (count // 2,), 0, 1 << 20) % (room + 1)
    sizes = sizes.at[donor].add(-moved).at[receiver].add(moved)
    items = jnp.searchsorted(jnp.cumsum(sizes), jnp.arange(rows * top), side="right").astype(jnp.int32)
    grid = items.reshape(top, rows).T
    grid = grid[jax.random.permutation(jax.random.fold_in(own, 1), rows)]
    turn = jax.random.randint(jax.random.fold_in(own, 2), (rows, 1), 0, top)
    return jnp.take_along_axis(grid, (jnp.arange(top)[None, :] + turn) % top, axis=1)


def portions_of(number_of, total, reach, skew, full):
    portions = [(1 << 20) // math.isqrt(grade ** skew) + 1 for grade in range(1, number_of + 1)]
    largest = reach if full else min(reach, max(-(-total // number_of), total * portions[0] // sum(portions)))
    least = 1 if total - largest >= number_of - 1 else 0
    holding, spare = [largest] + [least] * (number_of - 1), total - largest - least * (number_of - 1)
    while spare > 0:
        candidates = [i for i in range(1, number_of) if holding[i] < largest] or [i for i in range(1, number_of) if holding[i] < reach]
        mass, left = sum([portions[i] for i in candidates]), spare
        for i in candidates:
            addition = min(reach - holding[i], max(1, left * portions[i] // mass), spare)
            holding[i] = holding[i] + addition
            spare = spare - addition
    return np.array(holding)


def gaussian(rng, extent, width, reach, shards=(), held_as=jnp.bfloat16):
    array = jax.random.normal(rng, extent, jnp.float32) * width
    if len(shards) > 0:
        array = steps_of(rng, extent, shards, -0.22, 0.18) * array
    return jnp.clip(array, min=-reach, max=reach).astype(held_as)


def gaussian_with(own_key, extent, width, limit, pieces, heavy, held_as=jnp.bfloat16):
    result = width * jax.random.normal(own_key, extent, jnp.float32)
    if pieces:
        result = result * steps_of(own_key, extent, pieces, -0.22, 0.18)
    return jnp.clip(with_spikes(result, jax.random.fold_in(own_key, 3), *heavy), -limit, limit).astype(held_as)


def setup_inputs(seed: int = 0) -> dict:
    key_of = jax.random.split(jax.random.key(seed), 11)
    projected = gaussian(key_of[0], (3, LENGTH, D), 1.0, 6.0, ((1, 8), (2, 4)))
    stream = gaussian(key_of[1], (LENGTH, D), 1.0, 6.0, ((0, 8), (1, 4)))
    short_filter = gaussian(key_of[2], (3, TAPS, D), TAPS ** -0.5, 3.5, ((2, 4),), jnp.float32)
    long_filter = gaussian(key_of[3], (LENGTH, D), LENGTH ** -0.5, 0.1875, ((0, 8), (1, 4)), jnp.float32)
    skip_gain = jnp.clip(1.0 + 0.15 * jax.random.normal(key_of[4], (D,), jnp.float32), 0.25, 1.75)
    norm_gain = jnp.clip(1.0 + 0.15 * jax.random.normal(key_of[5], (D,), jnp.float32), 0.25, 1.75)
    gate_up = gaussian_with(key_of[6], (EXPERTS, D, 2, FF), D ** -0.5, 0.125, ((0, 8), (1, 4)), (1, 3, 4, 2.0))
    down_weight = gaussian(key_of[7], (EXPERTS, FF, D), FF ** -0.5, 0.15625, ((0, 8), (2, 4)))
    expert_ids_keys = jax.random.split(jax.random.fold_in(key_of[8], 1), LENGTH // TOK_DEV)
    expert_ids_turns = jax.random.permutation(jax.random.fold_in(key_of[8], 3), LENGTH // TOK_DEV)
    expert_ids = jax.vmap(lambda own, number: routed_block(jax.random.fold_in(key_of[8], 2), own, number, TOK_DEV, EXPERTS, TOP, CAP, 2))(expert_ids_keys, expert_ids_turns).reshape((LENGTH, TOP))
    gate_weights = jnp.clip(0.2 + 0.8 * jax.random.uniform(key_of[9], (LENGTH, TOP), jnp.float32) ** steps_of(key_of[9], (LENGTH, TOP), ((0, 8),), -0.2, 0.2), 0.2, 1.0)
    return {"projected": projected, "stream": stream, "short_filter": short_filter, "long_filter": long_filter, "skip_gain": skip_gain, "norm_gain": norm_gain, "gate_up": gate_up, "down_weight": down_weight, "expert_ids": expert_ids, "gate_weights": gate_weights}


def reference(projected, stream, short_filter, long_filter, skip_gain, norm_gain, gate_up, down_weight, expert_ids, gate_weights):
    values = projected.astype(jnp.float32)
    length = values.shape[1]
    mixed_short = short_filter[:, 0][:, None, :] * values
    for offset in range(1, TAPS):
        shifted = jnp.pad(values, ((0, 0), (offset, 0), (0, 0)))[:, :length]
        mixed_short = mixed_short + short_filter[:, offset][:, None, :] * shifted
    queries = mixed_short[0]
    key_side = mixed_short[1]
    valued = mixed_short[2]
    product = key_side * valued
    spectrum = jnp.fft.rfft(product, n=2 * length, axis=0) * jnp.fft.rfft(long_filter, n=2 * length, axis=0)
    convolved = jnp.fft.irfft(spectrum, n=2 * length, axis=0)[:length]
    mixed_long = queries * (convolved + skip_gain * product)
    residual = (stream.astype(jnp.float32) + mixed_long).astype(jnp.bfloat16)
    resid_float = residual.astype(jnp.float32)
    root_mean = jnp.sqrt(lax.optimization_barrier(jnp.sum(resid_float * resid_float, axis=1)) / D + 1e-06)
    normed = (resid_float / root_mean[:, None] * norm_gain).astype(jnp.bfloat16)
    block_ids_flat = expert_ids.reshape(N_SEQ, TOK_DEV * TOP)
    onehot = (block_ids_flat[:, :, None] == jnp.arange(EXPERTS, dtype=jnp.int32)[None, None, :]).astype(jnp.int32)
    slot_ids = lax.optimization_barrier(jnp.sum((jnp.cumsum(onehot, axis=1) - onehot) * onehot, axis=2)).astype(jnp.int32)
    block_ids = jnp.broadcast_to(jnp.arange(N_SEQ, dtype=jnp.int32)[:, None], block_ids_flat.shape)
    token_ids = block_ids * TOK_DEV + jnp.arange(TOK_DEV * TOP, dtype=jnp.int32)[None, :] // TOP
    slot_table = jnp.zeros((EXPERTS, N_SEQ, CAP), jnp.int32).at[block_ids_flat, block_ids, slot_ids].set(token_ids + 1)
    padded = jnp.concatenate([jnp.zeros((1, D), jnp.bfloat16), normed], axis=0)

    def one_expert(running, input_rows):
        sources, weights_in, output_weight = input_rows
        gathered = padded[sources.reshape(-1)].astype(jnp.float32).reshape(-1, N_EXP, D // N_EXP)
        blocked = weights_in.astype(jnp.float32).reshape(N_EXP, D // N_EXP, 2 * FF)
        partials = jnp.einsum('rbc,bcf->rbf', gathered, blocked)
        rounded = lax.optimization_barrier(partials.astype(jnp.bfloat16))
        totals = lax.optimization_barrier(jnp.sum(rounded.astype(jnp.float32), axis=1))
        hidden_state = (jax.nn.silu(totals[:, :FF]) * totals[:, FF:]).astype(jnp.bfloat16)
        final_output = jnp.dot(hidden_state, output_weight, preferred_element_type=jnp.float32).astype(jnp.bfloat16)
        return (running, final_output)
    unused, expert_out = lax.scan(one_expert, jnp.zeros((), jnp.float32), (slot_table, gate_up, down_weight))
    flat_out = expert_out.reshape(EXPERTS * N_SEQ * CAP, D)
    position = (block_ids_flat * (N_SEQ * CAP) + block_ids * CAP + slot_ids).reshape(N_SEQ * TOK_DEV, TOP)
    combined = jnp.zeros((length, D), jnp.float32)
    for pick_k in range(TOP):
        combined = combined + gate_weights[:, pick_k:pick_k + 1] * flat_out[position[:, pick_k]].astype(jnp.float32)
    return (resid_float + combined).astype(jnp.bfloat16)
```

```python
import math

import jax
import jax.numpy as jnp
from jax import lax
from jax.sharding import PartitionSpec as P


BF16 = jnp.bfloat16
F32 = jnp.float32


def shifted(value, axis, by):
    devices = lax.axis_size(axis)
    pairs = [(i, i + by) for i in range(devices) if 0 <= i + by < devices]
    return lax.ppermute(value, axis, pairs)


def flipped(value, axis, mask):
    return lax.ppermute(value, axis, [(i, i ^ mask) for i in range(lax.axis_size(axis))])


def rolled(value, axis, by):
    devices = lax.axis_size(axis)
    return lax.ppermute(value, axis, [(i, (i + by) % devices) for i in range(devices)])


def split_channels(value, me, count):
    rows, channels = value.shape
    width = channels // count
    pieces = []
    for k in range(count):
        piece = lax.dynamic_slice(value, (0, (me ^ k) * width), (rows, width))
        pieces.append(piece if k == 0 else flipped(piece, "seq", k))
    return jnp.concatenate(pieces, axis=0)


def join_channels(value, me, count):
    rows = value.shape[0] // count
    pieces = []
    for k in range(count):
        piece = value[k * rows : (k + 1) * rows]
        pieces.append(piece if k == 0 else flipped(piece, "seq", k))
    stacked = jnp.stack(pieces)
    columns = [lax.dynamic_index_in_dim(stacked, me ^ k, 0, keepdims=False) for k in range(count)]
    return jnp.concatenate(columns, axis=1)


def rotation_tables(length, block, me):
    period = 16 * length
    low = 16
    places = jnp.arange(length, dtype=jnp.int32) ^ (me * block)
    columns = 4 * places + 1
    high_rows = 4 * places[::low]
    low_rows = 4 * jnp.arange(low, dtype=jnp.int32) + 1
    unit = 2.0 * math.pi / period

    def angles(rows):
        turns = (rows[:, None] * columns[None, :]) % period
        value = unit * turns.astype(F32)
        return jnp.cos(value), jnp.sin(value)

    high_cos, high_sin = angles(high_rows)
    low_cos, low_sin = angles(low_rows)
    high_cos, high_sin = high_cos[:, None, :], high_sin[:, None, :]
    low_cos, low_sin = low_cos[None], low_sin[None]
    cos_table = (high_cos * low_cos - high_sin * low_sin).astype(BF16).reshape(length, length)
    sin_table = (high_sin * low_cos + high_cos * low_sin).astype(BF16).reshape(length, length)
    own = unit * columns.astype(F32)
    return cos_table, sin_table, jnp.cos(own)[:, None], jnp.sin(own)[:, None]


def dot(left, right):
    return jnp.dot(left, right, preferred_element_type=F32)


def local(
    projected,
    stream,
    short_filter,
    long_filter,
    skip_gain,
    norm_gain,
    gate_up,
    down_weight,
    expert_ids,
    gate_weights,
):
    seq_count = lax.axis_size("seq")
    exp_count = lax.axis_size("exp")
    me = lax.axis_index("seq")
    mine = lax.axis_index("exp")
    tok_rows = projected.shape[1]
    channels = projected.shape[2]
    tap_count = short_filter.shape[1]
    top_count = expert_ids.shape[1]
    model = channels * exp_count
    length = tok_rows * seq_count
    rounds = seq_count // 2
    cross = exp_count // 2

    earlier = shifted(projected[:, tok_rows - (tap_count - 1) :, :], "seq", 1)
    filter_whole = split_channels(long_filter.astype(BF16), me, seq_count)
    routing = jnp.concatenate([expert_ids.astype(F32).T, gate_weights.T], axis=0)
    routes = [routing]
    for _ in range(1, rounds):
        routes.append(rolled(routes[-1], "seq", 2))
    routes_other = [flipped(value, "seq", 1) for value in routes]

    extended = jnp.concatenate([earlier, projected], axis=1).astype(F32)
    mixed_short = short_filter[:, 0][:, None, :] * extended[:, tap_count - 1 :]
    for offset in range(1, tap_count):
        begin = tap_count - 1 - offset
        mixed_short = (
            mixed_short
            + short_filter[:, offset][:, None, :] * extended[:, begin : begin + tok_rows]
        )
    queries = mixed_short[0]
    product = mixed_short[1] * mixed_short[2]

    cos_table, sin_table, own_cos, own_sin = rotation_tables(length, tok_rows, me)
    filter_re = dot(cos_table, filter_whole)
    filter_im = -dot(sin_table, filter_whole)
    turned_re = (filter_re * own_cos - filter_im * own_sin) / length
    turned_im = (filter_re * own_sin + filter_im * own_cos) / length
    whole = split_channels(product.astype(BF16), me, seq_count)
    spec_re = dot(cos_table, whole)
    spec_im = -dot(sin_table, whole)
    joint_re = (spec_re * turned_re - spec_im * turned_im).astype(BF16)
    joint_im = (spec_re * turned_im + spec_im * turned_re).astype(BF16)
    result_long = dot(cos_table, joint_re) - dot(sin_table, joint_im)
    convolved = join_channels(result_long.astype(BF16), me, seq_count).astype(F32)
    mixed_long = queries * (convolved + skip_gain * product)
    residual = (stream.astype(F32) + mixed_long).astype(BF16)

    held = [residual]
    for _ in range(1, rounds):
        held.append(rolled(held[-1], "seq", 2))
    held_other = [flipped(value, "seq", 1) for value in held]

    local_experts = gate_up.shape[0]
    experts = local_experts * seq_count
    capacity = tok_rows * top_count * 4 // (experts * 3)
    share = capacity // exp_count
    core, place = mine % 2, mine // 2
    first_expert = (me * local_experts).astype(F32)
    expert_row = first_expert + jnp.arange(local_experts, dtype=F32)
    ahead = (
        lax.broadcasted_iota(jnp.int32, (tok_rows, tok_rows), 0)
        < lax.broadcasted_iota(jnp.int32, (tok_rows, tok_rows), 1)
    ).astype(BF16)

    def swapped_cores(value):
        return flipped(value, "exp", 1)

    def to_place(value, by):
        return rolled(value, "exp", 2 * by)

    def expert_chunk(blocks, tables):
        count = len(blocks)
        gathered = jnp.concatenate(blocks, axis=0)
        table = jnp.stack(tables)
        ids, weights = table[:, :top_count], table[:, top_count:]
        match = ids[:, None] == expert_row[None, :, None, None]
        hit = jnp.any(match, axis=2)
        picked = jnp.sum(jnp.where(match, weights[:, None], 0.0), axis=2)
        slot = dot(hit.astype(BF16).reshape(-1, tok_rows), ahead).astype(jnp.int32)
        slot = slot.reshape(count, local_experts, tok_rows)
        base = jnp.arange(count, dtype=jnp.int32)[:, None, None] * capacity
        code = jnp.where(hit, slot + base, -1).transpose(1, 0, 2).reshape(local_experts, 1, -1)
        picked = picked.transpose(1, 0, 2).reshape(local_experts, 1, -1)

        wide = gathered.astype(F32)
        squares = jnp.sum(wide * wide, axis=1)
        squares = squares + swapped_cores(squares)
        total_squares = squares
        for by in range(1, cross):
            total_squares = total_squares + to_place(squares, by)
        scale = lax.rsqrt(total_squares / model + 1e-06)

        shape = (cross, count, share)
        turn = (lax.broadcasted_iota(jnp.int32, shape, 0) + place) % cross
        inner = lax.broadcasted_iota(jnp.int32, shape, 1) * capacity + lax.broadcasted_iota(
            jnp.int32, shape, 2
        )

        def chosen(other):
            row_code = inner + (turn * 2 + (core ^ other)) * share
            return row_code.reshape(1, -1, 1) == code

        keep, send = chosen(0), chosen(1)

        def partial_of(mask):
            flat = mask.astype(BF16).reshape(-1, mask.shape[2])
            rows = (dot(flat, gathered) * norm_gain).astype(BF16)
            rows = rows.reshape(local_experts, -1, channels)
            return jnp.einsum(
                "enc,ecgf->engf", rows, gate_up, preferred_element_type=F32
            ).astype(BF16)

        sent = partial_of(send)
        arrived = swapped_cores(sent)
        kept = partial_of(keep)
        pair = kept.astype(F32) + arrived.astype(F32)
        pair = pair.reshape(local_experts, cross, count * share, *pair.shape[2:])
        totals = pair[:, 0]
        for by in range(1, cross):
            totals = totals + to_place(pair[:, by].astype(BF16), by).astype(F32)
        row_scale = jnp.sum(jnp.where(keep[:, : count * share], scale, 0.0), axis=2)
        totals = totals * row_scale[:, :, None, None]
        hidden = (jax.nn.silu(totals[:, :, 0]) * totals[:, :, 1]).astype(BF16)
        hidden_rows = [hidden] + [to_place(hidden, cross - by) for by in range(1, cross)]
        hidden_keep = jnp.concatenate(hidden_rows, axis=1)
        hidden_send = swapped_cores(hidden_keep)

        def combined(mask, rows):
            final = jnp.einsum("ent,etc->enc", rows, down_weight, preferred_element_type=F32)
            row_weight = jnp.sum(jnp.where(mask, picked, 0.0), axis=2)
            weighted = (final * row_weight[:, :, None]).astype(BF16).reshape(-1, channels)
            flat = mask.astype(BF16).reshape(-1, mask.shape[2])
            return lax.dot_general(
                flat, weighted, (((0,), (0,)), ((), ())), preferred_element_type=F32
            )

        total = combined(keep, hidden_keep) + combined(send, hidden_send)
        return total.reshape(count, tok_rows, channels)

    chunk_rounds = max(1, rounds // 2)
    own_row, other_row = [], []
    for begin in range(0, rounds, chunk_rounds):
        steps = range(begin, begin + chunk_rounds)
        blocks = [held[r] for r in steps] + [held_other[r] for r in steps]
        tables = [routes[r] for r in steps] + [routes_other[r] for r in steps]
        outcome = expert_chunk(blocks, tables)
        own_row += [outcome[i] for i in range(chunk_rounds)]
        other_row += [outcome[chunk_rounds + i] for i in range(chunk_rounds)]

    def part(r):
        return own_row[r] + flipped(other_row[r].astype(BF16), "seq", 1).astype(F32)

    if rounds > 1:
        moving = part(1)
        for r in range(2, rounds):
            moving = part(r) + rolled(moving.astype(BF16), "seq", 2).astype(F32)
        last = part(0) + rolled(moving.astype(BF16), "seq", 2).astype(F32)
    else:
        last = part(0)
    return (residual.astype(F32) + last).astype(BF16)


def solution(mesh):
    in_specs = (
        P(None, "seq", "exp"),
        P("seq", "exp"),
        P(None, None, "exp"),
        P("seq", "exp"),
        P("exp"),
        P("exp"),
        P("seq", "exp", None, None),
        P("seq", None, "exp"),
        P("seq", None),
        P("seq", None),
    )
    out_specs = P("seq", "exp")
    return jax.shard_map(local, mesh=mesh, in_specs=in_specs, out_specs=out_specs, check_vma=False)
```

```python
import math

import jax
import jax.numpy as jnp
from jax import lax
from jax.sharding import PartitionSpec as P


BF16 = jnp.bfloat16
F32 = jnp.float32


def shifted(value, axis, by):
    devices = lax.axis_size(axis)
    pairs = [(i, i + by) for i in range(devices) if 0 <= i + by < devices]
    return lax.ppermute(value, axis, pairs)


def flipped(value, axis, mask):
    return lax.ppermute(value, axis, [(i, i ^ mask) for i in range(lax.axis_size(axis))])


def rolled(value, axis, by):
    devices = lax.axis_size(axis)
    return lax.ppermute(value, axis, [(i, (i + by) % devices) for i in range(devices)])


def by_owner(value, count):
    rows, channels = value.shape
    return value.reshape(rows, count, channels // count).transpose(1, 0, 2)


def exchanged(value):
    return lax.all_to_all(value, "seq", split_axis=0, concat_axis=0, tiled=True)


def rotation_tables(length):
    period = 16 * length
    low = 16
    columns = 4 * jnp.arange(length, dtype=jnp.int32) + 1
    high_rows = 4 * low * jnp.arange(length // low, dtype=jnp.int32)
    low_rows = 4 * jnp.arange(low, dtype=jnp.int32) + 1
    unit = 2.0 * math.pi / period

    def angles(rows):
        turns = (rows[:, None] * columns[None, :]) % period
        value = unit * turns.astype(F32)
        return jnp.cos(value), jnp.sin(value)

    high_cos, high_sin = angles(high_rows)
    low_cos, low_sin = angles(low_rows)
    high_cos, high_sin = high_cos[:, None, :], high_sin[:, None, :]
    low_cos, low_sin = low_cos[None], low_sin[None]
    cos_table = (high_cos * low_cos - high_sin * low_sin).astype(BF16).reshape(length, length)
    sin_table = (high_sin * low_cos + high_cos * low_sin).astype(BF16).reshape(length, length)
    own = unit * columns.astype(F32)
    return cos_table, sin_table, jnp.cos(own)[:, None], jnp.sin(own)[:, None]


def after(value, done):
    return lax.optimization_barrier((value, done))[0]


def dot(left, right):
    return jnp.dot(left, right, preferred_element_type=F32)


def local(
    projected,
    stream,
    short_filter,
    long_filter,
    skip_gain,
    norm_gain,
    gate_up,
    down_weight,
    expert_ids,
    gate_weights,
):
    seq_count = lax.axis_size("seq")
    exp_count = lax.axis_size("exp")
    me = lax.axis_index("seq")
    mine = lax.axis_index("exp")
    tok_rows = projected.shape[1]
    channels = projected.shape[2]
    tap_count = short_filter.shape[1]
    top_count = expert_ids.shape[1]
    model = channels * exp_count
    length = tok_rows * seq_count
    rounds = seq_count // 2
    cross = exp_count // 2

    earlier = shifted(projected[:, tok_rows - (tap_count - 1) :, :], "seq", 1)
    coarse = lax.reduce_precision(gate_weights, 8, 7)
    routing = jnp.concatenate([expert_ids.astype(F32), coarse, gate_weights - coarse], axis=1).T
    width = channels // seq_count
    folded = -(-routing.size // width)
    folded = -(-folded // 16) * 16
    routing = jnp.pad(routing.reshape(-1), (0, folded * width - routing.size))
    routing = jnp.broadcast_to(routing.reshape(1, folded, width), (seq_count, folded, width))
    package = jnp.concatenate([by_owner(long_filter, seq_count), routing], axis=1).astype(BF16)
    package = exchanged(package)
    filter_whole = package[:, :tok_rows].reshape(length, width)
    routes = package[:, tok_rows:].astype(F32).reshape(seq_count, -1)[:, : 3 * top_count * tok_rows]
    routes = routes.reshape(seq_count, 3 * top_count, tok_rows)
    ids = routes[:, :top_count]
    weights = routes[:, top_count : 2 * top_count] + routes[:, 2 * top_count :]
    slots = jnp.arange(seq_count, dtype=jnp.int32)
    source = 2 * ((me // 2 - slots // 2) % rounds) + ((me % 2) ^ (slots % 2))
    picker = (source[:, None] == jnp.arange(seq_count, dtype=jnp.int32)[None, :])[:, :, None, None]
    ids = jnp.sum(jnp.where(picker, ids[None], 0.0), axis=1)
    weights = jnp.sum(jnp.where(picker, weights[None], 0.0), axis=1)

    extended = jnp.concatenate([earlier, projected], axis=1).astype(F32)
    mixed_short = short_filter[:, 0][:, None, :] * extended[:, tap_count - 1 :]
    for offset in range(1, tap_count):
        begin = tap_count - 1 - offset
        mixed_short = (
            mixed_short
            + short_filter[:, offset][:, None, :] * extended[:, begin : begin + tok_rows]
        )
    queries = mixed_short[0]
    product = mixed_short[1] * mixed_short[2]

    cos_table, sin_table, own_cos, own_sin = rotation_tables(length)
    filter_re = dot(cos_table, filter_whole)
    filter_im = -dot(sin_table, filter_whole)
    turned_re = (filter_re * own_cos - filter_im * own_sin) / length
    turned_im = (filter_re * own_sin + filter_im * own_cos) / length
    whole = exchanged(by_owner(product.astype(BF16), seq_count)).reshape(length, width)
    spec_re = dot(cos_table, whole)
    spec_im = -dot(sin_table, whole)
    joint_re = (spec_re * turned_re - spec_im * turned_im).astype(BF16)
    joint_im = (spec_re * turned_im + spec_im * turned_re).astype(BF16)
    result_long = dot(cos_table, joint_re) - dot(sin_table, joint_im)
    convolved = exchanged(result_long.astype(BF16).reshape(seq_count, tok_rows, width))
    convolved = convolved.transpose(1, 0, 2).reshape(tok_rows, channels).astype(F32)
    mixed_long = queries * (convolved + skip_gain * product)
    residual = (stream.astype(F32) + mixed_long).astype(BF16)

    held = [residual]
    for _ in range(1, rounds):
        held.append(rolled(held[-1], "seq", 2))
    held_other = [flipped(value, "seq", 1) for value in held]

    local_experts = gate_up.shape[0]
    experts = local_experts * seq_count
    capacity = tok_rows * top_count * 4 // (experts * 3)
    share = capacity // exp_count
    core, place = mine % 2, mine // 2
    first_expert = (me * local_experts).astype(F32)
    expert_row = first_expert + jnp.arange(local_experts, dtype=F32)
    ahead = (
        lax.broadcasted_iota(jnp.int32, (tok_rows, tok_rows), 0)
        < lax.broadcasted_iota(jnp.int32, (tok_rows, tok_rows), 1)
    ).astype(BF16)

    def swapped_cores(value):
        return flipped(value, "exp", 1)

    def to_place(value, by):
        return rolled(value, "exp", 2 * by)

    match = ids[:, None] == expert_row[None, :, None, None]
    hit = jnp.any(match, axis=2)
    picked = jnp.sum(jnp.where(match, weights[:, None], 0.0), axis=2)
    number = dot(hit.astype(BF16).reshape(-1, tok_rows), ahead).astype(jnp.int32)
    number = jnp.where(hit, number.reshape(hit.shape), -1)

    def table_of(first, count):
        base = jnp.arange(count, dtype=jnp.int32)[:, None, None] * capacity
        code = number[first : first + count]
        code = jnp.where(code < 0, -1, code + base).transpose(1, 0, 2)
        code = code.reshape(local_experts, 1, -1)
        shape = (2, cross, count, share)
        turn = [lax.broadcasted_iota(jnp.int32, shape, i) for i in range(4)]
        row_code = turn[2] * capacity + turn[3]
        row_code = row_code + (((turn[1] + place) % cross) * 2 + (core ^ turn[0])) * share
        mask = row_code.reshape(1, -1, 1) == code
        weight = picked[first : first + count].transpose(1, 0, 2).reshape(local_experts, 1, -1)
        row_weight = jnp.sum(jnp.where(mask, weight, 0.0), axis=2, keepdims=True)
        return mask, mask.astype(BF16).reshape(-1, mask.shape[2]), row_weight

    def multiplied(gathered, table):
        mask, flat, _ = table
        wide = gathered.astype(F32)
        squares = jnp.sum(wide * wide, axis=1)
        rows = (dot(flat, gathered) * norm_gain).astype(BF16)
        rows = rows.reshape(local_experts, -1, channels)
        partial = jnp.einsum("enc,ecgf->engf", rows, gate_up, preferred_element_type=F32)
        partial = partial.astype(BF16)
        half = partial.shape[1] // 2
        return partial[:, :half], partial[:, half:], squares

    def paired(kept, sent):
        pair = kept.astype(F32) + swapped_cores(sent).astype(F32)
        pair = pair.reshape(local_experts, cross, -1, *pair.shape[2:])
        return [pair[:, 0]] + [pair[:, by].astype(BF16) for by in range(1, cross)]

    def activated(pair, squares, table):
        totals = pair[0]
        for by in range(1, cross):
            totals = totals + to_place(pair[by], by).astype(F32)
        squares = squares + swapped_cores(squares)
        total_squares = squares
        for by in range(1, cross):
            total_squares = total_squares + to_place(squares, by)
        scale = lax.rsqrt(total_squares / model + 1e-06)
        row_scale = jnp.sum(jnp.where(table[0][:, : totals.shape[1]], scale, 0.0), axis=2)
        totals = totals * row_scale[:, :, None, None]
        return (jax.nn.silu(totals[:, :, 0]) * totals[:, :, 1]).astype(BF16)

    def shared(hidden):
        rows = [hidden] + [to_place(hidden, cross - by) for by in range(1, cross)]
        rows = jnp.concatenate(rows, axis=1)
        return jnp.concatenate([rows, swapped_cores(rows)], axis=1)

    def finished(rows, table):
        _, flat, row_weight = table
        final = jnp.einsum("ent,etc->enc", rows, down_weight, preferred_element_type=F32)
        weighted = (final * row_weight).astype(BF16).reshape(-1, channels)
        total = lax.dot_general(
            flat, weighted, (((0,), (0,)), ((), ())), preferred_element_type=F32
        )
        return total.reshape(-1, 2, tok_rows, channels)

    bounds = sorted({0, min(1, rounds), max(1, rounds - 1), rounds})
    spans = list(zip(bounds[:-1], bounds[1:]))
    tables = [table_of(2 * a, 2 * (b - a)) for a, b in spans]
    gathered = [
        jnp.concatenate([x for r in range(a, b) for x in (held[r], held_other[r])], axis=0)
        for a, b in spans
    ]
    products, pairs, hiddens = [], [], []
    for i, (a, b) in enumerate(spans):
        rows = gathered[i]
        if i == 1:
            hiddens.append(activated(pairs[0], products[0][2], tables[0]))
            rows = after(rows, hiddens[0])
        elif i > 1:
            rows = after(rows, pairs[i - 1])
        products.append(multiplied(rows, tables[i]))
        pairs.append(paired(*products[i][:2]))
    for i in range(len(hiddens), len(spans)):
        hiddens.append(activated(pairs[i], products[i][2], tables[i]))
    outcome = []
    for i in range(len(spans)):
        rows = shared(hiddens[i])
        if i == 0:
            rows = after(rows, pairs[-1])
        outcome.append(finished(rows, tables[i]))
    own_row = [o[r, 0] for o in outcome for r in range(o.shape[0])]
    other_row = [o[r, 1] for o in outcome for r in range(o.shape[0])]

    def part(r):
        return own_row[r] + flipped(other_row[r].astype(BF16), "seq", 1).astype(F32)

    if rounds > 1:
        moving = part(1)
        for r in range(2, rounds):
            moving = part(r) + rolled(moving.astype(BF16), "seq", 2).astype(F32)
        last = part(0) + rolled(moving.astype(BF16), "seq", 2).astype(F32)
    else:
        last = part(0)
    return (residual.astype(F32) + last).astype(BF16)


def solution(mesh):
    in_specs = (
        P(None, "seq", "exp"),
        P("seq", "exp"),
        P(None, None, "exp"),
        P("seq", "exp"),
        P("exp"),
        P("exp"),
        P("seq", "exp", None, None),
        P("seq", None, "exp"),
        P("seq", None),
        P("seq", None),
    )
    out_specs = P("seq", "exp")
    return jax.shard_map(local, mesh=mesh, in_specs=in_specs, out_specs=out_specs, check_vma=False)
```
